32 devices in a mesh: row: 4 (over y, x), col: 8 (over z, core).
Axes of the slice: x: 2, y: 2, z: 4, core: 2. Of those that a mesh axis runs over, the one named last changes fastest.
Arguments:
- queries: bfloat16 [3072, 1024], P(('row', 'col')), may hold values from -128 to 128
- keys: bfloat16 [3072, 128], P(('row', 'col')), may hold values from -4 to 4
- values: bfloat16 [3072, 128], P(('row', 'col')), may hold values from -6 to 6
- block_start: int32 [32], P(('row', 'col')), may hold values from 0 to 31, as said below
Outputs:
- attended: float32 [3072, 1024], P(('row', 'col'))
- log_total: float32 [3072, 8], P(('row', 'col'))
The draws below stay inside these ranges and needn't reach their ends.
Inputs may be any that keep to these rules, and one draw needn't show every extreme that they name: `block_start`: a permutation of 0 to 31.
All inputs are finite; a program needn't handle non-finite values.
Results may differ from the reference program's by a relative error of at most 0.0028.
Values may be sent and summed in bfloat16 or wider, within the bound.
No kernel may reach another device: no remote copies, remote signals or barrier semaphores. Data moves between devices by JAX's collectives and lax.ppermute only.
A program may use at most 64 MiB of HBM per device.

```python
import jax
import jax.numpy as jnp
from jax import lax

HD = 128
QH = 8
TOK_DEV = 96
BLOCKS = 32
TOKENS = 3072


def shared_keys(key):
    return jnp.clip(jax.random.normal(jax.random.fold_in(key, 11), (TOKENS, HD), jnp.float32), -4.0, 4.0)


def draw_keys(key, part):
    return shared_keys(key).astype(jnp.bfloat16)


def draw_block_start(key, part):
    return jax.random.permutation(jax.random.fold_in(key, 13), BLOCKS).astype(jnp.int32)


def draw_queries(key, part):
    sub_key = jax.random.fold_in(key, 12)
    result = jnp.clip(3.0 * jax.random.normal(sub_key, (TOKENS, QH * HD), jnp.float32), -12.0, 12.0)
    return result.astype(jnp.bfloat16)


def level_of(own_key, extent, pieces, least, largest):
    def one(dim, blocks):
        draws = jax.random.uniform(jax.random.fold_in(jax.random.fold_in(own_key, 6), dim), (blocks,), jnp.float32, least / len(pieces), largest / len(pieces))
        return jnp.repeat(jnp.exp(draws), extent[dim] // blocks).reshape((-1,) + (1,) * (len(extent) - dim - 1))

    factor_of = one(*pieces[0])
    for cut in pieces[1:]:
        factor_of = factor_of * one(*cut)
    return factor_of


def scatter_about(stream_key, shape, deviation, reach, cuts=(), kind=jnp.bfloat16):
    factor_of = level_of(stream_key, shape, cuts, -0.22, 0.18) if cuts else 1.0
    values = jax.random.normal(stream_key, shape, jnp.float32) * deviation * factor_of
    return jnp.minimum(jnp.maximum(values, -reach), reach).astype(kind)


def setup_inputs(seed: int = 0) -> dict:
    streams_of = jax.random.split(jax.random.key(seed), 5)
    return {
        "queries": draw_queries(jax.random.fold_in(streams_of[4], 71), 0),
        "keys": draw_keys(jax.random.fold_in(streams_of[4], 71), 0),
        "values": scatter_about(streams_of[2], (TOKENS, HD), 1.0, 6.0, ((0, 32),)),
        "block_start": draw_block_start(jax.random.fold_in(streams_of[4], 71), 0),
    }


def reference(queries, keys, values, block_start):
    scale = HD ** -0.5
    offsets = jnp.arange(TOK_DEV, dtype=jnp.int32)
    positions = (block_start[:, None] * TOK_DEV + offsets[None, :]).reshape(-1).astype(jnp.int32)
    query_blocks = queries.reshape(BLOCKS, TOK_DEV * QH, HD)

    def one_block(items):
        query_rows, begin_at = items
        row_pos = jnp.repeat(begin_at * TOK_DEV + offsets, QH)
        scores = jnp.dot(query_rows, keys.T, preferred_element_type=jnp.float32) * scale
        kept = positions[None, :] <= row_pos[:, None]
        scores = jnp.where(kept, scores, -1e30)
        peak = jnp.max(scores, axis=1)
        weights = jnp.where(kept, jnp.exp(scores - peak[:, None]), 0.0)
        total = jnp.sum(weights, axis=1)
        mixed = jnp.dot(weights.astype(jnp.bfloat16), values, preferred_element_type=jnp.float32)
        result = mixed / total[:, None]
        return result.reshape(TOK_DEV, QH * HD), (peak + jnp.log(total)).reshape(TOK_DEV, QH)

    attended, log_total = lax.map(one_block, (query_blocks, block_start))
    return attended.reshape(TOKENS, QH * HD), log_total.reshape(TOKENS, QH)
```

```python
import functools
import math

import jax
import jax.numpy as jnp
from jax import lax
from jax.experimental import pallas as pl
from jax.experimental.pallas import tpu as pltpu
from jax.sharding import PartitionSpec as P

NEG = -1e30
IDR = 8
VMEM = pl.BlockSpec(memory_space=pltpu.VMEM)
SMEM = pl.BlockSpec(memory_space=pltpu.SMEM)


def up8(n):
    return (n + IDR - 1) // IDR * IDR


def pack_kernel(start, k, v, out):
    tok, width = k.shape
    out[:tok, :width] = k[...]
    out[:tok, width:] = v[...]
    number = start[0].astype(jnp.float32)
    out[tok:, :] = jnp.full((IDR, 2 * width), number, jnp.float32).astype(jnp.bfloat16)


def pair_kernel(tok, mine, other, out):
    out[:tok, :] = mine[:tok, :]
    out[tok : 2 * tok, :] = other[:tok, :]
    row = lax.broadcasted_iota(jnp.int32, (IDR, out.shape[1]), 0)
    a = mine[tok:, :].astype(jnp.float32)
    b = other[tok:, :].astype(jnp.float32)
    out[2 * tok :, :] = jnp.where(row % 2 == 0, a, b).astype(jnp.bfloat16)


def base_kernel(tok, counts, *refs):
    out = refs[-1]
    at = 0
    source = []
    for count, ref in zip(counts, refs[:-1]):
        out[at : at + count * tok, :] = ref[: count * tok, :]
        source += [(ref, count)] * count
        at += count * tok
    row = lax.broadcasted_iota(jnp.int32, (IDR, out.shape[1]), 0)
    for first in range(0, out.shape[0] - at, IDR):
        ids = jnp.zeros((IDR, out.shape[1]), jnp.float32)
        for j in range(first, min(first + IDR, len(source))):
            ref, count = source[j]
            ids = jnp.where(row == j - first, ref[count * tok :, :].astype(jnp.float32), ids)
        out[at + first : at + first + IDR, :] = ids.astype(jnp.bfloat16)


def attend_kernel(tok, heads, blocks, per, start, q, *refs):
    n = len(refs) - 6
    bufs = refs[:n]
    out, log_total, qs, peak, total, accum = refs[n:]
    width = q.shape[1] // heads
    c = width ** (-0.5) * math.log2(math.e)
    for h in range(heads):
        qs[h * tok : (h + 1) * tok, :] = q[:, h * width : (h + 1) * width]
    me = start[0].astype(jnp.float32)
    keys = per * tok
    lane = lax.broadcasted_iota(jnp.int32, (1, keys), 1)
    group = heads // 2
    rows = group * tok
    ones = jnp.ones((keys, width), jnp.bfloat16)
    for b, buf in enumerate(bufs):
        for first in range(0, blocks, per):
            k = buf[first * tok : first * tok + keys, :width]
            v = buf[first * tok : first * tok + keys, width:]
            vv = jnp.concatenate([v, ones], axis=1)
            ids = jnp.zeros((1, keys), jnp.float32)
            tile = blocks * tok + first // IDR * IDR
            idrow = buf[tile : tile + IDR, :width].astype(jnp.float32)
            for j in range(per):
                at = first % IDR + j
                one = jnp.max(idrow[at : at + 1, :], axis=1, keepdims=True)
                ids = jnp.where(lane // tok == j, one, ids)
            kept = ids < me
            if b == 0 and first == 0:
                qi = lax.broadcasted_iota(jnp.int32, (tok, keys), 0)
                ki = lax.broadcasted_iota(jnp.int32, (tok, keys), 1)
                own = jnp.where(ki < tok, jnp.where(ki <= qi, 0.0, NEG), NEG)
                bias = jnp.where(kept & (lane >= tok), 0.0, own)
                bias = jnp.concatenate([bias] * group, axis=0)
            else:
                bias = jnp.where(kept, 0.0, NEG)
            for g in range(2):
                r = slice(g * rows, (g + 1) * rows)
                s = lax.dot_general(qs[r, :], k, (((1,), (1,)), ((), ())), preferred_element_type=jnp.float32)
                s = s * c + bias
                top = jnp.max(s, axis=1, keepdims=True)
                if b == 0 and first == 0:
                    new = top
                    w = jnp.exp2(s - new).astype(jnp.bfloat16)
                    mixed = jnp.dot(w, vv, preferred_element_type=jnp.float32)
                    accum[r, :] = mixed[:, :width]
                    total[r, :] = mixed[:, width:]
                else:
                    old = peak[r, :]
                    new = jnp.maximum(old, top)
                    w = jnp.exp2(s - new[:, :1]).astype(jnp.bfloat16)
                    mixed = jnp.dot(w, vv, preferred_element_type=jnp.float32)
                    alpha = jnp.exp2(old - new)
                    accum[r, :] = accum[r, :] * alpha + mixed[:, :width]
                    total[r, :] = total[r, :] * alpha + mixed[:, width:]
                peak[r, :] = jnp.broadcast_to(new, (rows, width))
    for h in range(heads):
        r = slice(h * tok, (h + 1) * tok)
        t = total[r, :]
        out[:, h * width : (h + 1) * width] = accum[r, :] / t
        lt = peak[r, :] * math.log(2.0) + jnp.log(t)
        log_total[h : h + 1, :] = lt.T[:1, :]


def call(kernel, out_shape, *args, smem=0, scratch=(), cost=None):
    many = isinstance(out_shape, list)
    return pl.pallas_call(
        kernel,
        out_shape=out_shape,
        in_specs=[SMEM] * smem + [VMEM] * (len(args) - smem),
        out_specs=[VMEM] * len(out_shape) if many else VMEM,
        scratch_shapes=list(scratch),
        cost_estimate=cost,
    )(*args)


def shifted(i, step, n):
    return i ^ step if n & (n - 1) == 0 else (i + step) % n


def local(row_size, col_size, queries, keys, values, block_start):
    tok, width = keys.shape
    heads = queries.shape[1] // width
    chips = col_size // 2
    bf16 = jnp.bfloat16

    def send(x, move):
        pairs = []
        for d in range(row_size * col_size):
            r, z, c = d // col_size, d % col_size // 2, d % 2
            r2, z2, c2 = move(r, z, c)
            pairs.append((d, r2 * col_size + z2 * 2 + c2))
        return lax.ppermute(x, ("row", "col"), pairs)

    def to_core(x):
        return send(x, lambda r, z, c: (r, z, c ^ 1))

    def shape(blocks):
        return jax.ShapeDtypeStruct((blocks * tok + up8(blocks), 2 * width), bf16)

    mine = call(pack_kernel, shape(1), block_start, keys, values, smem=1)
    other = to_core(mine)
    last = send(mine, lambda r, z, c: (r, shifted(z, chips - 1, chips), c))
    pair = call(functools.partial(pair_kernel, tok), shape(2), mine, other)
    messages = [mine, last]
    counts = [1, 1]
    for step in range(1, chips - 2, 2):
        messages.append(send(pair, lambda r, z, c: (r, shifted(z, step + c, chips), c)))
        counts.append(2)
    blocks = sum(counts)
    base = call(functools.partial(base_kernel, tok, counts), shape(blocks), *messages)
    pieces = [base]
    bits = row_size.bit_length() - 1
    for stage in range(bits):
        pieces += [send(p, lambda r, z, c: (r ^ (1 << (stage + c) % bits), z, c)) for p in pieces]
    every = []
    for p in pieces:
        every += [p, to_core(p)]
    per = min(blocks, 4)
    rows = heads * tok
    attended, log_total = call(
        functools.partial(attend_kernel, tok, heads, blocks, per),
        [jax.ShapeDtypeStruct((tok, heads * width), jnp.float32), jax.ShapeDtypeStruct((heads, tok), jnp.float32)],
        block_start,
        queries,
        *every,
        smem=1,
        scratch=[
            pltpu.VMEM((rows, width), bf16),
            pltpu.VMEM((rows, width), jnp.float32),
            pltpu.VMEM((rows, width), jnp.float32),
            pltpu.VMEM((rows, width), jnp.float32),
        ],
    )
    return attended, log_total.T


def solution(mesh):
    placed = P(("row", "col"), None)
    return jax.shard_map(
        functools.partial(local, mesh.shape["row"], mesh.shape["col"]),
        mesh=mesh,
        in_specs=(placed, placed, placed, P(("row", "col"))),
        out_specs=(placed, placed),
        check_vma=False,
    )
```
